256 devices in a mesh: expert: 32 (over z, y), etp: 8 (over x, core).
Axes of the slice: x: 4, y: 4, z: 8, core: 2. Of those that a mesh axis runs over, the one named last changes fastest.
Arguments:
- tokens: bfloat16 [32768, 2560], P(('expert', 'etp')), may hold values from -6 to 6
- grad_out: bfloat16 [32768, 2560], P(('expert', 'etp')), may hold values from -6 to 6
- router_weight: bfloat16 [2560, 32], replicated, may hold values from -0.125 to 0.125
- expert_choice: int32 [32768, 1], P(('expert', 'etp')), may hold values from 0 to 31; in each aligned block of 128 rows (0 to 127, 128 to 255, ...) at most 6 rows name the same one
- gate_pre: bfloat16 [32, 1536, 4096], P('expert', None, 'etp'), may hold values from -6 to 6
- up_pre: bfloat16 [32, 1536, 4096], P('expert', None, 'etp'), may hold values from -6 to 6
- w_gate: bfloat16 [32, 2560, 4096], P('expert', None, 'etp'), may hold values from -0.125 to 0.125
- w_up: bfloat16 [32, 2560, 4096], P('expert', None, 'etp'), may hold values from -0.125 to 0.125
- w_down: bfloat16 [32, 4096, 2560], P('expert', 'etp'), may hold values from -0.09375 to 0.09375
Outputs:
- token_grad: bfloat16 [32768, 2560], P(('expert', 'etp'))
- router_grad: float32 [2560, 32], replicated
The draws below stay inside these ranges and needn't reach their ends.
Inputs may be any that keep to these rules, and one draw needn't show every extreme that they name: `expert_choice`: within the 128 tokens of one device no expert is chosen more than 6 times, and in every draw some expert is chosen exactly 6 times by the tokens of some device.
All inputs are finite; a program needn't handle non-finite values.
Results may differ from the reference program's by a relative error of at most 0.015.
Values may be sent and summed in bfloat16 or wider, within the bound.
No kernel may reach another device: no remote copies, remote signals or barrier semaphores. Data moves between devices by JAX's collectives and lax.ppermute only.
A program may use at most 128 MiB of HBM per device.

```python
import math
import jax
import jax.numpy as jnp
import numpy as np
from jax import lax

D = 2560
F = 4096
TOK_DEV = 128
EXPERTS = 32
CAP = 6
SLOTS = 1536
TOKENS = 32768
N_EXPERT = 32
N_ETP = 8


def block_scale(key, extent, pieces, least, largest):
    level, own = 1.0, jax.random.fold_in(key, 6)
    for dim, blocks in pieces:
        draws = jnp.exp(jax.random.uniform(jax.random.fold_in(own, dim), (blocks,), jnp.float32, least / len(pieces), largest / len(pieces)))
        level = level * jnp.repeat(draws, extent[dim] // blocks).reshape([-1 if axis == dim else 1 for axis in range(len(extent))])
    return level


def shared_out(stream_key, own, number, rows, number_of, top, most, skew):
    order = jax.random.permutation(stream_key, number_of)
    crowded, common = load_shares(number_of, rows * top, most, skew, True), load_shares(number_of, rows * top, most, skew, False)
    places = jnp.arange(number_of)

    def named(sizes, turn):
        used = int((sizes > 0).sum())
        fixed = max(1, used // 4)
        moved = fixed + (places - fixed + turn * (used - fixed)) % max(1, number_of - fixed)
        return jnp.zeros((number_of,), jnp.int32).at[order[jnp.where(places < fixed, places, moved)]].set(jnp.asarray(sizes, jnp.int32))

    sizes = jnp.where(number % 4 == 0, named(crowded, number // 4), named(common, number - number // 4 - 1))
    mixed = jax.random.permutation(jax.random.fold_in(own, 3), number_of)
    donor, sink = mixed[0:number_of // 2 * 2:2], mixed[1:number_of // 2 * 2:2]
    margin = jnp.minimum(sizes[donor] - 1, most - sizes[sink]) // 2
    margin = jnp.where((donor == order[0]) | (sink == order[0]) | (sizes[sink] == 0), 0, jnp.maximum(margin, 0))
    moved = jax.random.randint(jax.random.fold_in(own, 4), (number_of // 2,), 0, 1 << 20) % (margin + 1)
    sizes = sizes.at[donor].add(-moved).at[sink].add(moved)
    labels = jnp.searchsorted(jnp.cumsum(sizes), jnp.arange(rows * top), side="right").astype(jnp.int32)
    table = labels.reshape(top, rows).T
    table = table[jax.random.permutation(jax.random.fold_in(own, 1), rows)]
    turn = jax.random.randint(jax.random.fold_in(own, 2), (rows, 1), 0, top)
    return jnp.take_along_axis(table, (jnp.arange(top)[None, :] + turn) % top, axis=1)


def load_shares(count, total, most, lean, full):
    portions = [(1 << 20) // math.isqrt(standing ** lean) + 1 for standing in range(1, count + 1)]
    largest = most if full else min(most, max(-(-total // count), total * portions[0] // sum(portions)))
    least = 1 if total - largest >= count - 1 else 0
    given, rest = [largest] + [least] * (count - 1), total - largest - least * (count - 1)
    while rest > 0:
        free = [i for i in range(1, count) if given[i] < largest] or [i for i in range(1, count) if given[i] < most]
        whole, left = sum([portions[i] for i in free]), rest
        for i in free:
            extra = min(most - given[i], max(1, left * portions[i] // whole), rest)
            given[i] = given[i] + extra
            rest = rest - extra
    return np.array(given)


def scatter_about(key, shape, deviation, most, cuts=(), kind=jnp.bfloat16):
    entries = deviation * jax.random.normal(key, shape, jnp.float32)
    if cuts:
        entries = entries * block_scale(key, shape, cuts, -0.22, 0.18)
    return jnp.clip(entries, -most, most).astype(kind)


def setup_inputs(seed: int = 0) -> dict:
    seeds = jax.random.split(jax.random.key(seed), 10)
    tokens = scatter_about(seeds[0], (TOKENS, D), 1.0, 6.0, ((0, 256),))
    grad_out = scatter_about(seeds[1], (TOKENS, D), 1.0, 6.0, ((0, 256),))
    router_weight = scatter_about(seeds[2], (D, EXPERTS), D ** -0.5, 0.125)
    expert_choice_keys = jax.random.split(jax.random.fold_in(seeds[3], 1), TOKENS // TOK_DEV)
    expert_choice_turns = jax.random.permutation(jax.random.fold_in(seeds[3], 3), TOKENS // TOK_DEV)
    expert_choice = jax.vmap(lambda own, number: shared_out(jax.random.fold_in(seeds[3], 2), own, number, TOK_DEV, EXPERTS, 1, CAP, 2))(expert_choice_keys, expert_choice_turns).reshape((TOKENS, 1))
    gate_pre = scatter_about(seeds[4], (EXPERTS, SLOTS, F), 1.0, 6.0, ((0, 32), (2, 8)))
    up_pre = scatter_about(seeds[5], (EXPERTS, SLOTS, F), 1.0, 6.0, ((0, 32), (2, 8)))
    w_gate = scatter_about(seeds[6], (EXPERTS, D, F), D ** -0.5, 0.125, ((0, 32), (2, 8)))
    w_up = scatter_about(seeds[7], (EXPERTS, D, F), D ** -0.5, 0.125, ((0, 32), (2, 8)))
    w_down = scatter_about(seeds[8], (EXPERTS, F, D), F ** -0.5, 0.09375, ((0, 32), (1, 8)))
    return {"tokens": tokens, "grad_out": grad_out, "router_weight": router_weight, "expert_choice": expert_choice, "gate_pre": gate_pre, "up_pre": up_pre, "w_gate": w_gate, "w_up": w_up, "w_down": w_down}


def reference(tokens, grad_out, router_weight, expert_choice, gate_pre, up_pre, w_gate, w_up, w_down):
    chosen_ids = expert_choice[:, 0]
    picked = chosen_ids[:, None] == jnp.arange(EXPERTS, dtype=jnp.int32)[None, :]
    logits = jnp.dot(tokens, router_weight, preferred_element_type=jnp.float32)
    score = jax.nn.sigmoid(jnp.sum(jnp.where(picked, logits, jnp.float32(0.0)), axis=1))
    counts = picked.astype(jnp.int32).reshape(N_EXPERT * N_ETP, TOK_DEV, EXPERTS)
    earlier = jnp.cumsum(counts, axis=1) - counts
    position = jnp.sum(earlier * counts, axis=2).reshape(TOKENS)
    block = jnp.arange(TOKENS, dtype=jnp.int32) // TOK_DEV
    row = ((block % N_ETP) * N_EXPERT + block // N_ETP) * CAP + position
    shard = F // N_ETP

    def one_expert(input_grad, packed):
        index, gate, upper, wgate, wup, wdown = packed
        here = chosen_ids == index
        target = jnp.where(here, row, SLOTS).astype(jnp.int32)
        sent = jnp.zeros((SLOTS, D), jnp.bfloat16).at[target].set(grad_out, mode="drop")
        d_hidden = jnp.dot(sent, wdown.T, preferred_element_type=jnp.float32)
        gate_f = gate.astype(jnp.float32)
        up_f = upper.astype(jnp.float32)
        sig = jax.nn.sigmoid(gate_f)
        d_gate = (d_hidden * up_f * sig * (1.0 + gate_f * (1.0 - sig))).astype(jnp.bfloat16)
        d_up = (d_hidden * gate_f * sig).astype(jnp.bfloat16)
        gate_parts = d_gate.astype(jnp.float32).reshape(SLOTS, N_ETP, shard)
        up_parts = d_up.astype(jnp.float32).reshape(SLOTS, N_ETP, shard)
        wgate_f = wgate.astype(jnp.float32).reshape(D, N_ETP, shard)
        wup_f = wup.astype(jnp.float32).reshape(D, N_ETP, shard)
        parts = jnp.einsum('skf,dkf->ksd', gate_parts, wgate_f) + jnp.einsum('skf,dkf->ksd', up_parts, wup_f)
        rounded = lax.optimization_barrier(parts.astype(jnp.bfloat16)).astype(jnp.float32)
        slot_grad = jnp.sum(rounded, axis=0).astype(jnp.bfloat16)
        fetched = slot_grad[jnp.minimum(row, SLOTS - 1).astype(jnp.int32)]
        return jnp.where(here[:, None], fetched, input_grad), None

    start = jnp.zeros((TOKENS, D), jnp.bfloat16)
    experts_idx = jnp.arange(EXPERTS, dtype=jnp.int32)
    input_grad, _ = lax.scan(one_expert, start, (experts_idx, gate_pre, up_pre, w_gate, w_up, w_down))
    grad_f = input_grad.astype(jnp.float32)
    inputs = tokens.astype(jnp.float32)
    d_logit = jnp.sum(inputs * grad_f, axis=1) * score * (1.0 - score)
    column = router_weight.astype(jnp.float32).T[chosen_ids]
    token_grad = (score[:, None] * grad_f + d_logit[:, None] * column).astype(jnp.bfloat16)
    weighted = jnp.where(picked, d_logit[:, None], jnp.float32(0.0))
    router_grad = jnp.dot(inputs.T, weighted, precision=lax.Precision.HIGHEST, preferred_element_type=jnp.float32)
    return token_grad, router_grad
```

```python
import jax
import jax.numpy as jnp
from jax import lax
from jax.sharding import PartitionSpec as P


def local(tokens, grad_out, router_weight, expert_choice, gate_pre, up_pre, w_gate, w_up, w_down):
    width = tokens.shape[1]
    experts = router_weight.shape[1]
    n_expert = lax.axis_size("expert")
    n_etp = lax.axis_size("etp")
    capacity = gate_pre.shape[1] // (n_expert * n_etp)
    contract = (((1,), (1,)), ((), ()))
    chosen_ids = expert_choice[:, 0]
    picked = chosen_ids[:, None] == jnp.arange(experts, dtype=jnp.int32)[None, :]
    logits = jnp.dot(tokens, router_weight, preferred_element_type=jnp.float32)
    score = jax.nn.sigmoid(jnp.sum(jnp.where(picked, logits, 0.0), axis=1))
    counts = picked.astype(jnp.int32)
    earlier = jnp.cumsum(counts, axis=0) - counts
    position = jnp.sum(earlier * counts, axis=1)
    target = chosen_ids * capacity + position
    placed = jnp.arange(experts * capacity, dtype=jnp.int32)[:, None] == target[None, :]
    onehot = placed.astype(jnp.bfloat16)
    outgoing = jnp.dot(onehot, grad_out, preferred_element_type=jnp.float32).astype(jnp.bfloat16)
    own = lax.all_to_all(outgoing, "expert", split_axis=0, concat_axis=0, tiled=True)
    arrived = lax.all_gather(own, "etp", axis=0, tiled=True)
    d_hidden = lax.dot_general(arrived, w_down[0], contract, preferred_element_type=jnp.float32)
    gate_f = gate_pre[0].astype(jnp.float32)
    up_f = up_pre[0].astype(jnp.float32)
    sig = jax.nn.sigmoid(gate_f)
    d_gate = (d_hidden * up_f * sig * (1.0 + gate_f * (1.0 - sig))).astype(jnp.bfloat16)
    d_up = (d_hidden * gate_f * sig).astype(jnp.bfloat16)
    terms = (
        lax.dot_general(d_gate, w_gate[0], contract, preferred_element_type=jnp.float32)
        + lax.dot_general(d_up, w_up[0], contract, preferred_element_type=jnp.float32)
    ).astype(jnp.bfloat16)
    summed = lax.psum_scatter(terms, "etp", scatter_dimension=0, tiled=True)
    returned = lax.all_to_all(summed, "expert", split_axis=0, concat_axis=0, tiled=True)
    fetched = lax.dot_general(
        onehot, returned, (((0,), (0,)), ((), ())), preferred_element_type=jnp.float32
    )
    inputs = tokens.astype(jnp.float32)
    d_logit = jnp.sum(inputs * fetched, axis=1) * score * (1.0 - score)
    column = lax.dot_general(
        picked.astype(jnp.bfloat16), router_weight, contract, preferred_element_type=jnp.float32
    )
    token_grad = (score[:, None] * fetched + d_logit[:, None] * column).astype(jnp.bfloat16)
    weighted = jnp.where(picked, d_logit[:, None], 0.0)
    local_terms = lax.dot_general(
        weighted, inputs, (((0,), (0,)), ((), ())), precision=lax.Precision.HIGHEST, preferred_element_type=jnp.float32
    )
    mine = lax.all_to_all(local_terms.reshape(n_etp, experts // n_etp, width), "etp", split_axis=0, concat_axis=0, tiled=True)
    mine = jnp.sum(mine, axis=0)
    mine = lax.psum(mine, "expert")
    router_grad = lax.all_gather(mine, "etp", axis=0, tiled=True).T
    return (token_grad, router_grad)


def solution(mesh):
    placed = (
        P(("expert", "etp"), None),
        P(("expert", "etp"), None),
        P(),
        P(("expert", "etp"), None),
        P("expert", None, "etp"),
        P("expert", None, "etp"),
        P("expert", None, "etp"),
        P("expert", None, "etp"),
        P("expert", "etp", None),
    )
    return jax.shard_map(
        local,
        mesh=mesh,
        in_specs=placed,
        out_specs=(P(("expert", "etp"), None), P()),
        check_vma=False,
    )
```

```python
import functools

import jax
import jax.numpy as jnp
from jax import lax
from jax.experimental import pallas as pl
from jax.experimental.pallas import tpu as pltpu
from jax.sharding import PartitionSpec as P

CAP = 6
PIECES = 4
GROUPS = 3
TILE = 8
NT = (((1,), (1,)), ((), ()))
TN = (((0,), (0,)), ((), ()))
NN = (((1,), (0,)), ((), ()))
F32 = jnp.float32
BF16 = jnp.bfloat16
PARAMS = pltpu.CompilerParams(vmem_limit_bytes=24 * 2**20)
COLUMNS = 512
COST = pl.CostEstimate(flops=0, transcendentals=0, bytes_accessed=2**20)


def iota(shape, axis):
    return lax.broadcasted_iota(jnp.int32, shape, axis)


def dot(a, b, dims=NN):
    return lax.dot_general(a, b, dims, preferred_element_type=F32)


def target_row(choice, experts):
    count = choice.shape[1]
    picked = (iota((experts, count), 0) == choice).astype(BF16)
    before = (iota((count, count), 0) < iota((count, count), 1)).astype(BF16)
    earlier = dot(picked, before)
    position = jnp.sum(picked.astype(F32) * earlier, axis=0, keepdims=True)
    return choice * CAP + position.astype(jnp.int32)


def hot_rows(target, peers, groups, piece):
    shape = (peers, len(groups) * TILE, target.shape[1])
    row = iota(shape, 1)
    slot = iota(shape, 0) * CAP + groups[0] * 2 + (row >> 3) * 2 + (row & 1)
    hit = (slot == target.reshape(1, 1, -1)) & (((row >> 1) & (PIECES - 1)) == piece)
    return jnp.where(hit, 1.0, 0.0).reshape(-1, target.shape[1]).astype(BF16)


def pack_rows(rows, target, peers, groups):
    width = rows.shape[1] // PIECES
    total = 0.0
    for piece in range(PIECES):
        total = total + dot(hot_rows(target, peers, groups, piece), rows[:, piece * width : (piece + 1) * width])
    return total.astype(BF16)


def pack_kernel(experts, groups, choice_ref, rows_ref, out_ref):
    target = target_row(choice_ref[...], experts)
    out_ref[...] = pack_rows(rows_ref[...], target, experts, groups)


def pack(choice, rows, experts, groups, name):
    width = rows.shape[1] // PIECES
    return pl.pallas_call(
        functools.partial(pack_kernel, experts, groups),
        out_shape=jax.ShapeDtypeStruct((experts * len(groups) * TILE, width), BF16),
        compiler_params=PARAMS,
        cost_estimate=COST,
        name=name,
    )(choice, rows)


def unpack_kernel(groups, packed_ref, *outs):
    width = packed_ref.shape[1]
    take = packed_ref.shape[0] // len(outs)
    rows = outs[0].shape[0]
    target = iota((1, rows), 1)
    for piece in range(PIECES):
        hot = hot_rows(target, rows // CAP, groups, piece)
        for half, out in enumerate(outs):
            part = packed_ref[half * take : (half + 1) * take, :]
            out[:, piece * width : (piece + 1) * width] = dot(hot, part, TN).astype(BF16)


def unpack(packed, groups, slots, halves, name):
    width = packed.shape[1] * PIECES
    return pl.pallas_call(
        functools.partial(unpack_kernel, groups),
        out_shape=[jax.ShapeDtypeStruct((slots // halves, width), BF16)] * halves,
        compiler_params=PARAMS,
        cost_estimate=COST,
        name=name,
    )(packed)


def expert_kernel(counts, ids_ref, *refs):
    total = sum(len(c) for c in counts)
    pieces, (gate, up, down, wg, wu) = refs[:total], refs[total : total + 5]
    outs = refs[total + 5 : total + 5 + 2 * len(counts)]
    lhs_ref, gate_ref, up_ref, down_ref, wg_ref, wu_ref, out_ref, dg_ref, du_ref, in_sem, out_sem = refs[total + 5 + len(outs) :]
    slots, width = outs[0].shape
    copies, at, number = [], 0, 0
    for j, chip in enumerate(counts):
        mine = []
        for rows in chip:
            mine.append(pltpu.make_async_copy(pieces[number], lhs_ref.at[pl.ds(at, rows)], in_sem.at[number]))
            at, number = at + rows, number + 1
        if j == 0:
            mine.append(pltpu.make_async_copy(down, down_ref, in_sem.at[total]))
        copies.append(mine)
    gates = []
    for i in range(len(outs)):
        spot = pl.ds(i * slots, slots)
        gates.append(pltpu.make_async_copy(gate.at[ids_ref[i]], gate_ref.at[spot], in_sem.at[total + 3 + 2 * i]))
        gates.append(pltpu.make_async_copy(up.at[ids_ref[i]], up_ref.at[spot], in_sem.at[total + 4 + 2 * i]))
    late = [pltpu.make_async_copy(wg, wg_ref, in_sem.at[total + 1]), pltpu.make_async_copy(wu, wu_ref, in_sem.at[total + 2])]
    for copy in copies[0]:
        copy.start()
    for copy in copies[0]:
        copy.wait()
    for copy in gates + late + sum(copies[1:], []):
        copy.start()
    last = []
    for j in range(len(counts)):
        spot = pl.ds(j * 2 * slots, 2 * slots)
        if j > 0:
            for copy in copies[j]:
                copy.wait()
        hidden = dot(lhs_ref[spot, :], down_ref[...], NT)
        for copy in gates[4 * j : 4 * j + 4]:
            copy.wait()
        gate_f = gate_ref[spot, :].astype(F32)
        up_f = up_ref[spot, :].astype(F32)
        sig = jax.nn.sigmoid(gate_f)
        dg_ref[...] = (hidden * up_f * sig * (1.0 + gate_f * (1.0 - sig))).astype(BF16)
        du_ref[...] = (hidden * gate_f * sig).astype(BF16)
        if j == 0:
            for copy in late:
                copy.wait()
        for tile in range(width // COLUMNS):
            cols = pl.ds(tile * COLUMNS, COLUMNS)
            terms = dot(dg_ref[...], wg_ref[cols, :], NT) + dot(du_ref[...], wu_ref[cols, :], NT)
            out_ref[spot, cols] = terms.astype(BF16)
        for i in range(2 * j, 2 * j + 2):
            copy = pltpu.make_async_copy(out_ref.at[pl.ds(i * slots, slots)], outs[i], out_sem.at[i])
            copy.start()
            last.append(copy)
    for copy in last:
        copy.wait()


def expert(ids, chips, gate, up, down_w, gate_w, up_w, name):
    width = chips[0][0].shape[1]
    slots, hidden = gate.shape[1:]
    blocks = 2 * len(chips)
    counts = tuple(tuple(piece.shape[0] for piece in chip) for chip in chips)
    pieces = [piece for chip in chips for piece in chip]
    vmem = lambda *shape: pltpu.VMEM(shape, BF16)
    anywhere = pl.BlockSpec(memory_space=pl.ANY)
    return pl.pallas_call(
        functools.partial(expert_kernel, counts),
        in_specs=[pl.BlockSpec(memory_space=pltpu.SMEM)] + [anywhere] * (len(pieces) + 5),
        out_specs=[anywhere] * blocks,
        out_shape=[jax.ShapeDtypeStruct((slots, width), BF16)] * blocks,
        scratch_shapes=[
            vmem(blocks * slots, width), vmem(blocks * slots, hidden), vmem(blocks * slots, hidden),
            vmem(hidden, width), vmem(width, hidden), vmem(width, hidden),
            vmem(blocks * slots, width), vmem(2 * slots, hidden), vmem(2 * slots, hidden),
            pltpu.SemaphoreType.DMA((len(pieces) + 3 + 2 * blocks,)), pltpu.SemaphoreType.DMA((blocks,)),
        ],
        compiler_params=pltpu.CompilerParams(vmem_limit_bytes=44 * 2**20),
        cost_estimate=COST,
        name=name,
    )(ids, *pieces, gate, up, down_w, gate_w, up_w)


def token_kernel(count, router_ref, *refs):
    halves = len(refs[-2:])
    out_ref, column_ref = refs[-2:]
    router = router_ref[...].astype(F32)
    column = 0.0
    for half in range(halves):
        parts = refs[half * count : (half + 1) * count]
        total = parts[0][...].astype(F32)
        for part in parts[1:]:
            total = total + part[...].astype(F32)
        grad = total.astype(BF16).astype(F32)
        tok = refs[2 * count + half][...].astype(F32)
        score = jax.nn.sigmoid(jnp.sum(tok * router, axis=1, keepdims=True))
        d_logit = jnp.sum(tok * grad, axis=1, keepdims=True) * score * (1.0 - score)
        token_grad = (score * grad + d_logit * router).astype(BF16)
        column = column + jnp.sum(d_logit * tok, axis=0, keepdims=True)
        rows = token_grad.shape[0]
        take = out_ref.shape[0] // halves
        out_ref[half * take : (half + 1) * take, :] = pack_rows(
            token_grad, iota((1, rows), 1), rows // CAP, tuple(range(GROUPS))
        )
    column_ref[...] = column


def token_math(parts, tok, router, name):
    rows, width = tok[0].shape
    return pl.pallas_call(
        functools.partial(token_kernel, len(parts[0])),
        out_shape=[
            jax.ShapeDtypeStruct((2 * rows // CAP * GROUPS * TILE, width // PIECES), BF16),
            jax.ShapeDtypeStruct((1, width), F32),
        ],
        compiler_params=PARAMS,
        cost_estimate=COST,
        name=name,
    )(router, *parts[0], *parts[1], *tok)


def final_kernel(experts, choice_ref, packed_ref, out_ref):
    target = target_row(choice_ref[...], experts)
    width = packed_ref.shape[1]
    for piece in range(PIECES):
        hot = hot_rows(target, experts, tuple(range(GROUPS)), piece)
        out_ref[:, piece * width : (piece + 1) * width] = dot(hot, packed_ref[...], TN).astype(BF16)


def final(choice, packed, experts, name):
    width = packed.shape[1] * PIECES
    return pl.pallas_call(
        functools.partial(final_kernel, experts),
        out_shape=jax.ShapeDtypeStruct((choice.shape[1], width), BF16),
        compiler_params=PARAMS,
        cost_estimate=COST,
        name=name,
    )(choice, packed)


def exchange(x, axis, parts):
    shaped = x.reshape(parts, x.shape[0] // parts, x.shape[1])
    return lax.all_to_all(shaped, axis, split_axis=0, concat_axis=0, tiled=True).reshape(x.shape)


def after(x, *gates):
    return lax.optimization_barrier((x, *gates))[0]


def local(tokens, grad_out, router_weight, expert_choice, gate_pre, up_pre, w_gate, w_up, w_down):
    width = tokens.shape[1]
    experts = router_weight.shape[1]
    n_expert = lax.axis_size("expert")
    n_etp = lax.axis_size("etp")
    chips = n_etp // 2
    choice = expert_choice.reshape(1, -1)
    hidden = gate_pre.shape[2]
    slots = gate_pre.shape[1] // n_etp
    gate = gate_pre.reshape(n_etp, slots, hidden)
    up = up_pre.reshape(n_etp, slots, hidden)
    weights = (w_down[0], w_gate[0], w_up[0])
    mine = lax.axis_index("etp")
    core = mine % 2
    chip = mine // 2
    router = lax.dynamic_index_in_dim(router_weight.T, lax.axis_index("expert"), 0)

    def shift(x, by):
        return lax.ppermute(x, "etp", [(i, ((i // 2 + by) % chips) * 2 + i % 2) for i in range(n_etp)])

    def swap(x):
        return lax.ppermute(x, "etp", [(i, i ^ 1) for i in range(n_etp)])

    def ids(*hops):
        at = [(chip + by) % chips * 2 for by in hops]
        return jnp.stack([place for a in at for place in (a + core, a + 1 - core)]).astype(jnp.int32)

    def add(*parts):
        return sum(part.astype(F32) for part in parts).astype(BF16)

    def low(x):
        return x[: x.shape[0] // 2]

    def high(x):
        return x[x.shape[0] // 2 :]

    every = tuple(range(GROUPS))
    sent = pack(choice, grad_out, experts, every, "pack_grad")
    arrived = exchange(sent, "expert", n_expert)
    sent_tok = pack(choice, after(tokens, sent), experts, every, "pack_tok")
    halves = unpack(arrived, every, slots, 2, "unpack_grad")

    left = [shift(half, 1) for half in halves]
    right = [shift(half, -1) for half in reversed(halves)][::-1]
    packed_tok = exchange(after(sent_tok, halves[0]), "expert", n_expert)
    own = [after(halves[0], sent_tok), halves[1]]
    keep, other = expert(ids(0), [own + [swap(half) for half in halves]], gate, up, *weights, "expert_own")
    keep_r = swap(other)
    left[0], right[1] = after(left[0], keep), after(right[1], keep)
    far = [shift(left[0], 1), shift(right[1], -1)]
    left_x, right_x = [swap(half) for half in left], [swap(half) for half in right]
    lk, lo, rk, ro = expert(ids(-1, 1), [left + left_x, right + right_x], gate, up, *weights, "expert_sides")
    lr, rr = swap(after(lo, packed_tok)), swap(ro)
    far_rows = [after(far[0], lk), far[1], swap(far[0]), swap(far[1])]
    fk, fo = expert(ids(2), [far_rows], gate, up, *weights, "expert_far")
    fr = swap(fo)

    to_left = [shift(add(low(lk), low(lr)), -1), None]
    to_right = [None, shift(add(high(rk), high(rr)), 1)]
    sums = add(low(fk), low(fr)), add(high(fk), high(fr))
    via_right, via_left = shift(sums[0], 1), shift(sums[1], -1)
    tok = unpack(after(packed_tok, *sums), every, slots, 2, "unpack_tok")
    to_right[0] = shift(add(low(after(rk, tok[0], to_left[0], to_right[1])), low(rr), via_right), 1)
    to_left[1] = shift(add(high(after(lk, tok[0], to_left[0], to_right[1])), high(lr), via_left), -1)
    parts = [[half(keep), half(keep_r), to_right[h], to_left[h]] for h, half in enumerate((low, high))]
    back, column = token_math(parts, tok, router, "token_math")
    returned = exchange(back, "expert", n_expert)
    token_grad = final(choice, returned, experts, "final")

    bit = 1
    while bit < n_etp:
        column = column + lax.ppermute(column, "etp", [(i, i ^ bit) for i in range(n_etp)])
        bit *= 2
    spread = jnp.broadcast_to(after(column, returned).reshape(1, TILE, width // TILE), (n_expert, TILE, width // TILE))
    spread = lax.all_to_all(spread, "expert", split_axis=0, concat_axis=0, tiled=True)
    return (token_grad, spread.reshape(experts, width).T)


def solution(mesh):
    placed = (
        P(("expert", "etp"), None),
        P(("expert", "etp"), None),
        P(),
        P(("expert", "etp"), None),
        P("expert", None, "etp"),
        P("expert", None, "etp"),
        P("expert", None, "etp"),
        P("expert", None, "etp"),
        P("expert", "etp", None),
    )
    return jax.shard_map(
        local,
        mesh=mesh,
        in_specs=placed,
        out_specs=(P(("expert", "etp"), None), P()),
        check_vma=False,
    )
```

```python
import functools

import jax
import jax.numpy as jnp
from jax import lax
from jax.experimental import pallas as pl
from jax.experimental.pallas import tpu as pltpu
from jax.sharding import PartitionSpec as P

CAP = 6
PIECES = 4
GROUPS = 3
TILE = 8
NT = (((1,), (1,)), ((), ()))
TN = (((0,), (0,)), ((), ()))
NN = (((1,), (0,)), ((), ()))
F32 = jnp.float32
BF16 = jnp.bfloat16
PARAMS = pltpu.CompilerParams(vmem_limit_bytes=24 * 2**20)
COLUMNS = 512
HOPS = (0, -1, 1, 2)
COST = pl.CostEstimate(flops=0, transcendentals=0, bytes_accessed=2**20)


def iota(shape, axis):
    return lax.broadcasted_iota(jnp.int32, shape, axis)


def dot(a, b, dims=NN):
    return lax.dot_general(a, b, dims, preferred_element_type=F32)


def target_row(choice, experts):
    count = choice.shape[1]
    picked = (iota((experts, count), 0) == choice).astype(BF16)
    before = (iota((count, count), 0) < iota((count, count), 1)).astype(BF16)
    earlier = dot(picked, before)
    position = jnp.sum(picked.astype(F32) * earlier, axis=0, keepdims=True)
    return choice * CAP + position.astype(jnp.int32)


def hot_rows(target, peers, groups, piece):
    shape = (peers, len(groups) * TILE, target.shape[1])
    row = iota(shape, 1)
    slot = iota(shape, 0) * CAP + groups[0] * 2 + (row >> 3) * 2 + (row & 1)
    hit = (slot == target.reshape(1, 1, -1)) & (((row >> 1) & (PIECES - 1)) == piece)
    return jnp.where(hit, 1.0, 0.0).reshape(-1, target.shape[1]).astype(BF16)


def pack_rows(rows, target, peers, groups):
    width = rows.shape[1] // PIECES
    total = 0.0
    for piece in range(PIECES):
        total = total + dot(hot_rows(target, peers, groups, piece), rows[:, piece * width : (piece + 1) * width])
    return total.astype(BF16)


def pack_kernel(experts, groups, choice_ref, rows_ref, out_ref):
    target = target_row(choice_ref[...], experts)
    out_ref[...] = pack_rows(rows_ref[...], target, experts, groups)


def pack(choice, rows, experts, groups, name):
    width = rows.shape[1] // PIECES
    return pl.pallas_call(
        functools.partial(pack_kernel, experts, groups),
        out_shape=jax.ShapeDtypeStruct((experts * len(groups) * TILE, width), BF16),
        compiler_params=PARAMS,
        cost_estimate=COST,
        name=name,
    )(choice, rows)


def unpack_kernel(groups, packed_ref, *outs):
    width = packed_ref.shape[1]
    take = packed_ref.shape[0] // len(outs)
    rows = outs[0].shape[0]
    target = iota((1, rows), 1)
    for piece in range(PIECES):
        hot = hot_rows(target, rows // CAP, groups, piece)
        for half, out in enumerate(outs):
            part = packed_ref[half * take : (half + 1) * take, :]
            out[:, piece * width : (piece + 1) * width] = dot(hot, part, TN).astype(BF16)


def unpack(packed, groups, slots, halves, name):
    width = packed.shape[1] * PIECES
    return pl.pallas_call(
        functools.partial(unpack_kernel, groups),
        out_shape=[jax.ShapeDtypeStruct((slots // halves, width), BF16)] * halves,
        compiler_params=PARAMS,
        cost_estimate=COST,
        name=name,
    )(packed)


def expert_kernel(first, counts, ids_ref, *refs):
    total = sum(len(c) for c in counts)
    pieces, (gate_ref, up_ref, down_ref, wg_ref, wu_ref) = refs[:total], refs[total : total + 5]
    outs = refs[total + 5 : total + 5 + 2 * len(counts)]
    lhs_ref, out_ref, dg_ref, du_ref, in_sem, out_sem = refs[total + 5 + len(outs) :]
    slots, width = outs[0].shape
    copies, at, number = [], 0, 0
    for chip in counts:
        for rows in chip:
            copies.append(pltpu.make_async_copy(pieces[number], lhs_ref.at[pl.ds(at, rows)], in_sem.at[number]))
            at, number = at + rows, number + 1
    for copy in copies:
        copy.start()
    last, number = [], 0
    for j, chip in enumerate(counts):
        spot = pl.ds(j * 2 * slots, 2 * slots)
        for _ in chip:
            copies[number].wait()
            number += 1
        hidden = dot(lhs_ref[spot, :], down_ref[...], NT)
        own, peer = ids_ref[2 * (first + j)], ids_ref[2 * (first + j) + 1]
        gate = jnp.concatenate([gate_ref[own], gate_ref[peer]], axis=0).astype(F32)
        up = jnp.concatenate([up_ref[own], up_ref[peer]], axis=0).astype(F32)
        sig = jax.nn.sigmoid(gate)
        dg_ref[...] = (hidden * up * sig * (1.0 + gate * (1.0 - sig))).astype(BF16)
        du_ref[...] = (hidden * gate * sig).astype(BF16)

        def tile(at):
            cols = pl.ds(at, COLUMNS)
            terms = dot(dg_ref[...], wg_ref[cols, :], NT) + dot(du_ref[...], wu_ref[cols, :], NT)
            out_ref[spot, cols] = terms.astype(BF16)

        @pl.loop(0, width // COLUMNS)
        def _(i):
            tile(pl.multiple_of(i * COLUMNS, COLUMNS))

        for i in range(2 * j, 2 * j + 2):
            copy = pltpu.make_async_copy(out_ref.at[pl.ds(i * slots, slots)], outs[i], out_sem.at[i])
            copy.start()
            last.append(copy)
    for copy in last:
        copy.wait()


def expert(ids, first, chips, gate, up, down_w, gate_w, up_w, name):
    width = chips[0][0].shape[1]
    slots, hidden = gate.shape[1:]
    blocks = 2 * len(chips)
    counts = tuple(tuple(piece.shape[0] for piece in chip) for chip in chips)
    pieces = [piece for chip in chips for piece in chip]
    vmem = lambda *shape: pltpu.VMEM(shape, BF16)
    anywhere = pl.BlockSpec(memory_space=pl.ANY)
    held = pl.BlockSpec(memory_space=pltpu.VMEM)
    return pl.pallas_call(
        functools.partial(expert_kernel, first, counts),
        in_specs=[pl.BlockSpec(memory_space=pltpu.SMEM)] + [anywhere] * len(pieces) + [held] * 5,
        out_specs=[anywhere] * blocks,
        out_shape=[jax.ShapeDtypeStruct((slots, width), BF16)] * blocks,
        scratch_shapes=[
            vmem(blocks * slots, width), vmem(blocks * slots, width), vmem(2 * slots, hidden), vmem(2 * slots, hidden),
            pltpu.SemaphoreType.DMA((len(pieces),)), pltpu.SemaphoreType.DMA((blocks,)),
        ],
        compiler_params=pltpu.CompilerParams(vmem_limit_bytes=24 * 2**20),
        cost_estimate=pl.CostEstimate(flops=0, transcendentals=0, bytes_accessed=2**20),
        name=name,
    )(ids, *pieces, gate, up, down_w, gate_w, up_w)


def add_kernel(spots, *refs):
    parts, out_ref, held, sem = refs[: len(spots)], refs[len(spots)], refs[len(spots) + 1 : -1], refs[-1]
    copies = []
    for i, (start, part) in enumerate(zip(spots, parts)):
        copies.append(pltpu.make_async_copy(part.at[pl.ds(start, held[i].shape[0])], held[i], sem.at[i]))
    for copy in copies:
        copy.start()
    for copy in copies:
        copy.wait()
    out_ref[...] = sum(ref[...].astype(F32) for ref in held).astype(BF16)


def add(rows, name, *parts):
    width = parts[0][0].shape[1]
    return pl.pallas_call(
        functools.partial(add_kernel, tuple(start for _, start in parts)),
        in_specs=[pl.BlockSpec(memory_space=pl.ANY)] * len(parts),
        out_shape=jax.ShapeDtypeStruct((rows, width), BF16),
        scratch_shapes=[pltpu.VMEM((rows, width), BF16)] * len(parts) + [pltpu.SemaphoreType.DMA((len(parts),))],
        compiler_params=pltpu.CompilerParams(vmem_limit_bytes=12 * 2**20),
        cost_estimate=COST,
        name=name,
    )(*[part for part, _ in parts])


def token_kernel(router_ref, keep_ref, keep_r_ref, *refs):
    parts, toks, (out_ref, column_ref) = refs[:4], refs[4:6], refs[6:]
    router = router_ref[...].astype(F32)
    column = 0.0
    rows = toks[0].shape[0]
    take = out_ref.shape[0] // 2
    for half in range(2):
        spot = slice(half * rows, (half + 1) * rows)
        total = keep_ref[spot, :].astype(F32) + keep_r_ref[spot, :].astype(F32)
        for part in parts[2 * half : 2 * half + 2]:
            total = total + part[...].astype(F32)
        grad = total.astype(BF16).astype(F32)
        tok = toks[half][...].astype(F32)
        score = jax.nn.sigmoid(jnp.sum(tok * router, axis=1, keepdims=True))
        d_logit = jnp.sum(tok * grad, axis=1, keepdims=True) * score * (1.0 - score)
        token_grad = (score * grad + d_logit * router).astype(BF16)
        column = column + jnp.sum(d_logit * tok, axis=0, keepdims=True)
        out_ref[half * take : (half + 1) * take, :] = pack_rows(
            token_grad, iota((1, rows), 1), rows // CAP, tuple(range(GROUPS))
        )
    column_ref[...] = column


def token_math(kept, parts, tok, router, name):
    rows, width = tok[0].shape
    return pl.pallas_call(
        token_kernel,
        out_shape=[
            jax.ShapeDtypeStruct((2 * rows // CAP * GROUPS * TILE, width // PIECES), BF16),
            jax.ShapeDtypeStruct((1, width), F32),
        ],
        compiler_params=PARAMS,
        cost_estimate=COST,
        name=name,
    )(router, *kept, *parts[0], *parts[1], *tok)


def final_kernel(experts, choice_ref, packed_ref, out_ref):
    target = target_row(choice_ref[...], experts)
    width = packed_ref.shape[1]
    for piece in range(PIECES):
        hot = hot_rows(target, experts, tuple(range(GROUPS)), piece)
        out_ref[:, piece * width : (piece + 1) * width] = dot(hot, packed_ref[...], TN).astype(BF16)


def final(choice, packed, experts, name):
    width = packed.shape[1] * PIECES
    return pl.pallas_call(
        functools.partial(final_kernel, experts),
        out_shape=jax.ShapeDtypeStruct((choice.shape[1], width), BF16),
        compiler_params=PARAMS,
        cost_estimate=COST,
        name=name,
    )(choice, packed)


def exchange(x, axis, parts, name):
    shaped = x.reshape(parts, x.shape[0] // parts, x.shape[1])
    with jax.named_scope(name):
        shaped = lax.all_to_all(shaped, axis, split_axis=0, concat_axis=0, tiled=True)
    return shaped.reshape(x.shape)


def after(x, *gates):
    return lax.optimization_barrier((x, *gates))[0]


def local(tokens, grad_out, router_weight, expert_choice, gate_pre, up_pre, w_gate, w_up, w_down):
    width = tokens.shape[1]
    experts = router_weight.shape[1]
    n_expert = lax.axis_size("expert")
    n_etp = lax.axis_size("etp")
    chips = n_etp // 2
    choice = expert_choice.reshape(1, -1)
    hidden = gate_pre.shape[2]
    slots = gate_pre.shape[1] // n_etp
    gate = gate_pre.reshape(n_etp, slots, hidden)
    up = up_pre.reshape(n_etp, slots, hidden)
    weights = (w_down[0], w_gate[0], w_up[0])
    mine = lax.axis_index("etp")
    core = mine % 2
    chip = mine // 2
    router = lax.dynamic_index_in_dim(router_weight.T, lax.axis_index("expert"), 0)
    near = (chip + jnp.array(HOPS, jnp.int32)) % chips * 2
    ids = jnp.stack([near + core, near + 1 - core], axis=1).reshape(-1).astype(jnp.int32)
    choice, ids, router = lax.optimization_barrier((choice, ids, router))

    def shift(x, by, name):
        with jax.named_scope(name):
            return lax.ppermute(x, "etp", [(i, ((i // 2 + by) % chips) * 2 + i % 2) for i in range(n_etp)])

    def swap(x, name):
        with jax.named_scope(name):
            return lax.ppermute(x, "etp", [(i, i ^ 1) for i in range(n_etp)])

    every = tuple(range(GROUPS))
    sent = pack(choice, grad_out, experts, every, "pack_grad")
    arrived = exchange(sent, "expert", n_expert, "grads")
    sent_tok = pack(choice, after(tokens, sent), experts, every, "pack_tok")
    halves = unpack(after(arrived, sent_tok), every, slots, 2, "unpack_grad")

    left = [shift(part, 1, f"left{i}") for i, part in enumerate(halves)]
    right = [shift(halves[i], -1, f"right{i}") for i in (1, 0)][::-1]
    own_x = [swap(part, f"own_x{i}") for i, part in enumerate(halves)]
    packed_tok = exchange(after(sent_tok, own_x[0]), "expert", n_expert, "toks")
    own = [after(halves[0], sent_tok), halves[1]]
    keep, other = expert(ids, 0, [own + own_x], gate, up, *weights, "expert_own")
    keep_r = swap(other, "own_sum")
    left[0], right[1] = after(left[0], keep), after(right[1], keep)
    far = [shift(left[0], 1, "far0"), shift(right[1], -1, "far1")]
    left_x = [swap(part, f"left_x{i}") for i, part in enumerate(left)]
    right_x = [swap(part, f"right_x{i}") for i, part in enumerate(right)]
    lk, lo, rk, ro = expert(ids, 1, [left + left_x, right + right_x], gate, up, *weights, "expert_sides")
    lr, rr = swap(lo, "left_sum"), swap(ro, "right_sum")
    half = slots // 2
    first = add(half, "sum_left0", (lk, 0), (lr, 0)), add(half, "sum_right1", (rk, half), (rr, half))
    far = [after(far[0], lk), after(far[1], lk)]
    far_x = [swap(part, f"far_x{i}") for i, part in enumerate(far)]
    far = [after(far[0], *first), far[1]]
    fk, fo = expert(ids, 3, [far + far_x], gate, up, *weights, "expert_far")
    fr = swap(after(fo, packed_tok), "far_sum")

    to_left = [shift(first[0], -1, "to_left0"), None]
    to_right = [None, shift(first[1], 1, "to_right1")]
    sums = add(half, "sum_far0", (fk, 0), (fr, 0)), add(half, "sum_far1", (fk, half), (fr, half))
    via_right, via_left = shift(sums[0], 1, "via_right"), shift(sums[1], -1, "via_left")
    tok = unpack(after(packed_tok, *sums), every, slots, 2, "unpack_tok")
    gated_r, gated_l, *_ = lax.optimization_barrier((rk, lk, tok[0], to_left[0], to_right[1]))
    to_right[0] = shift(add(half, "sum_right0", (gated_r, 0), (rr, 0), (via_right, 0)), 1, "to_right0")
    to_left[1] = shift(add(half, "sum_left1", (gated_l, half), (lr, half), (via_left, 0)), -1, "to_left1")
    parts = [[to_right[h], to_left[h]] for h in range(2)]
    back, column = token_math([keep, keep_r], parts, tok, router, "token_math")
    returned = exchange(back, "expert", n_expert, "back")
    token_grad = final(choice, returned, experts, "final")

    bit = 1
    while bit < n_etp:
        column = column + lax.ppermute(column, "etp", [(i, i ^ bit) for i in range(n_etp)])
        bit *= 2
    spread = jnp.broadcast_to(after(column, returned).reshape(1, TILE, width // TILE), (n_expert, TILE, width // TILE))
    spread = lax.all_to_all(spread, "expert", split_axis=0, concat_axis=0, tiled=True)
    return (token_grad, spread.reshape(experts, width).T)


def solution(mesh):
    placed = (
        P(("expert", "etp"), None),
        P(("expert", "etp"), None),
        P(),
        P(("expert", "etp"), None),
        P("expert", None, "etp"),
        P("expert", None, "etp"),
        P("expert", None, "etp"),
        P("expert", None, "etp"),
        P("expert", "etp", None),
    )
    return jax.shard_map(
        local,
        mesh=mesh,
        in_specs=placed,
        out_specs=(P(("expert", "etp"), None), P()),
        check_vma=False,
    )
```

```python
import functools

import jax
import jax.numpy as jnp
from jax import lax
from jax.experimental import pallas as pl
from jax.experimental.pallas import tpu as pltpu
from jax.sharding import PartitionSpec as P

CAP = 6
PIECES = 4
GROUPS = 3
TILE = 8
NT = (((1,), (1,)), ((), ()))
TN = (((0,), (0,)), ((), ()))
NN = (((1,), (0,)), ((), ()))
F32 = jnp.float32
BF16 = jnp.bfloat16
PARAMS = pltpu.CompilerParams(vmem_limit_bytes=24 * 2**20)
COLUMNS = 512
HOPS = (0, -1, 1, 2)
COST = pl.CostEstimate(flops=0, transcendentals=0, bytes_accessed=2**20)


def iota(shape, axis):
    return lax.broadcasted_iota(jnp.int32, shape, axis)


def dot(a, b, dims=NN):
    return lax.dot_general(a, b, dims, preferred_element_type=F32)


def target_row(choice, experts):
    count = choice.shape[1]
    picked = (iota((experts, count), 0) == choice).astype(BF16)
    before = (iota((count, count), 0) < iota((count, count), 1)).astype(BF16)
    earlier = dot(picked, before)
    position = jnp.sum(picked.astype(F32) * earlier, axis=0, keepdims=True)
    return choice * CAP + position.astype(jnp.int32)


def hot_rows(target, peers, groups, piece):
    shape = (peers, len(groups) * TILE, target.shape[1])
    row = iota(shape, 1)
    slot = iota(shape, 0) * CAP + groups[0] * 2 + (row >> 3) * 2 + (row & 1)
    hit = (slot == target.reshape(1, 1, -1)) & (((row >> 1) & (PIECES - 1)) == piece)
    return jnp.where(hit, 1.0, 0.0).reshape(-1, target.shape[1]).astype(BF16)


def pack_rows(rows, target, peers, groups):
    width = rows.shape[1] // PIECES
    total = 0.0
    for piece in range(PIECES):
        total = total + dot(hot_rows(target, peers, groups, piece), rows[:, piece * width : (piece + 1) * width])
    return total.astype(BF16)


def pack_kernel(experts, groups, choice_ref, rows_ref, out_ref):
    target = target_row(choice_ref[...], experts)
    out_ref[...] = pack_rows(rows_ref[...], target, experts, groups)


def pack(choice, rows, experts, groups, name):
    width = rows.shape[1] // PIECES
    return pl.pallas_call(
        functools.partial(pack_kernel, experts, groups),
        out_shape=jax.ShapeDtypeStruct((experts * len(groups) * TILE, width), BF16),
        compiler_params=PARAMS,
        cost_estimate=COST,
        name=name,
    )(choice, rows)


def unpack_kernel(groups, packed_ref, *outs):
    width = packed_ref.shape[1]
    take = packed_ref.shape[0] // len(outs)
    rows = outs[0].shape[0]
    target = iota((1, rows), 1)
    for piece in range(PIECES):
        hot = hot_rows(target, rows // CAP, groups, piece)
        for half, out in enumerate(outs):
            part = packed_ref[half * take : (half + 1) * take, :]
            out[:, piece * width : (piece + 1) * width] = dot(hot, part, TN).astype(BF16)


def unpack(packed, groups, slots, halves, name):
    width = packed.shape[1] * PIECES
    return pl.pallas_call(
        functools.partial(unpack_kernel, groups),
        out_shape=[jax.ShapeDtypeStruct((slots // halves, width), BF16)] * halves,
        compiler_params=PARAMS,
        cost_estimate=COST,
        name=name,
    )(packed)


def expert_kernel(first, counts, ids_ref, *refs):
    total = sum(len(c) for c in counts)
    pieces, (gate_ref, up_ref, down_ref, wg_ref, wu_ref) = refs[:total], refs[total : total + 5]
    outs = refs[total + 5 : total + 5 + 2 * len(counts)]
    lhs_ref, out_ref, dg_ref, du_ref, in_sem, out_sem = refs[total + 5 + len(outs) :]
    slots, width = outs[0].shape
    copies, at, number = [], 0, 0
    for chip in counts:
        for rows in chip:
            copies.append(pltpu.make_async_copy(pieces[number], lhs_ref.at[pl.ds(at, rows)], in_sem.at[number]))
            at, number = at + rows, number + 1
    for copy in copies:
        copy.start()
    last, number = [], 0
    for j, chip in enumerate(counts):
        spot = pl.ds(j * 2 * slots, 2 * slots)
        for _ in chip:
            copies[number].wait()
            number += 1
        hidden = dot(lhs_ref[spot, :], down_ref[...], NT)
        own, peer = ids_ref[2 * (first + j)], ids_ref[2 * (first + j) + 1]
        gate = jnp.concatenate([gate_ref[own], gate_ref[peer]], axis=0).astype(F32)
        up = jnp.concatenate([up_ref[own], up_ref[peer]], axis=0).astype(F32)
        sig = jax.nn.sigmoid(gate)
        dg_ref[...] = (hidden * up * sig * (1.0 + gate * (1.0 - sig))).astype(BF16)
        du_ref[...] = (hidden * gate * sig).astype(BF16)

        def tile(at):
            cols = pl.ds(at, COLUMNS)
            terms = dot(dg_ref[...], wg_ref[cols, :], NT) + dot(du_ref[...], wu_ref[cols, :], NT)
            out_ref[spot, cols] = terms.astype(BF16)

        @pl.loop(0, width // COLUMNS)
        def _(i):
            tile(pl.multiple_of(i * COLUMNS, COLUMNS))

        for i in range(2 * j, 2 * j + 2):
            copy = pltpu.make_async_copy(out_ref.at[pl.ds(i * slots, slots)], outs[i], out_sem.at[i])
            copy.start()
            last.append(copy)
    for copy in last:
        copy.wait()


def expert(ids, first, chips, gate, up, down_w, gate_w, up_w, name):
    width = chips[0][0].shape[1]
    slots, hidden = gate.shape[1:]
    blocks = 2 * len(chips)
    counts = tuple(tuple(piece.shape[0] for piece in chip) for chip in chips)
    pieces = [piece for chip in chips for piece in chip]
    vmem = lambda *shape: pltpu.VMEM(shape, BF16)
    anywhere = pl.BlockSpec(memory_space=pl.ANY)
    held = pl.BlockSpec(memory_space=pltpu.VMEM)
    return pl.pallas_call(
        functools.partial(expert_kernel, first, counts),
        in_specs=[pl.BlockSpec(memory_space=pltpu.SMEM)] + [anywhere] * len(pieces) + [held] * 5,
        out_specs=[anywhere] * blocks,
        out_shape=[jax.ShapeDtypeStruct((slots, width), BF16)] * blocks,
        scratch_shapes=[
            vmem(blocks * slots, width), vmem(blocks * slots, width), vmem(2 * slots, hidden), vmem(2 * slots, hidden),
            pltpu.SemaphoreType.DMA((len(pieces),)), pltpu.SemaphoreType.DMA((blocks,)),
        ],
        compiler_params=pltpu.CompilerParams(vmem_limit_bytes=24 * 2**20),
        cost_estimate=pl.CostEstimate(flops=0, transcendentals=0, bytes_accessed=2**20),
        name=name,
    )(ids, *pieces, gate, up, down_w, gate_w, up_w)


def add_kernel(spots, *refs):
    parts, out_ref, held, sem = refs[: len(spots)], refs[len(spots)], refs[len(spots) + 1 : -1], refs[-1]
    copies = []
    for i, (start, part) in enumerate(zip(spots, parts)):
        copies.append(pltpu.make_async_copy(part.at[pl.ds(start, held[i].shape[0])], held[i], sem.at[i]))
    for copy in copies:
        copy.start()
    for copy in copies:
        copy.wait()
    out_ref[...] = sum(ref[...].astype(F32) for ref in held).astype(BF16)


def add(rows, name, *parts):
    width = parts[0][0].shape[1]
    return pl.pallas_call(
        functools.partial(add_kernel, tuple(start for _, start in parts)),
        in_specs=[pl.BlockSpec(memory_space=pl.ANY)] * len(parts),
        out_shape=jax.ShapeDtypeStruct((rows, width), BF16),
        scratch_shapes=[pltpu.VMEM((rows, width), BF16)] * len(parts) + [pltpu.SemaphoreType.DMA((len(parts),))],
        compiler_params=pltpu.CompilerParams(vmem_limit_bytes=12 * 2**20),
        cost_estimate=COST,
        name=name,
    )(*[part for part, _ in parts])


def token_kernel(router_ref, keep_ref, keep_r_ref, *refs):
    parts, toks, (out_ref, column_ref) = refs[:4], refs[4:6], refs[6:]
    router = router_ref[...].astype(F32)
    column, grads = 0.0, []
    rows = toks[0].shape[0]
    take = out_ref.shape[0] // 2
    for half in range(2):
        spot = slice(half * rows, (half + 1) * rows)
        total = keep_ref[spot, :].astype(F32) + keep_r_ref[spot, :].astype(F32)
        for part in parts[2 * half : 2 * half + 2]:
            total = total + part[...].astype(F32)
        grad = total.astype(BF16).astype(F32)
        tok = toks[half][...].astype(F32)
        score = jax.nn.sigmoid(jnp.sum(tok * router, axis=1, keepdims=True))
        d_logit = jnp.sum(tok * grad, axis=1, keepdims=True) * score * (1.0 - score)
        token_grad = (score * grad + d_logit * router).astype(BF16)
        column = column + jnp.sum(d_logit * tok, axis=0, keepdims=True)
        grads.append(token_grad)
    column_ref[...] = column
    width = out_ref.shape[1]
    packed = [0.0, 0.0]
    for piece in range(PIECES):
        hot = hot_rows(iota((1, rows), 1), rows // CAP, tuple(range(GROUPS)), piece)
        for half in range(2):
            packed[half] = packed[half] + dot(hot, grads[half][:, piece * width : (piece + 1) * width])
    for half in range(2):
        out_ref[half * take : (half + 1) * take, :] = packed[half].astype(BF16)


def token_math(kept, parts, tok, router, name):
    rows, width = tok[0].shape
    return pl.pallas_call(
        token_kernel,
        out_shape=[
            jax.ShapeDtypeStruct((2 * rows // CAP * GROUPS * TILE, width // PIECES), BF16),
            jax.ShapeDtypeStruct((1, width), F32),
        ],
        compiler_params=PARAMS,
        cost_estimate=COST,
        name=name,
    )(router, *kept, *parts[0], *parts[1], *tok)


def final_kernel(experts, choice_ref, packed_ref, out_ref):
    target = target_row(choice_ref[...], experts)
    width = packed_ref.shape[1]
    for piece in range(PIECES):
        hot = hot_rows(target, experts, tuple(range(GROUPS)), piece)
        out_ref[:, piece * width : (piece + 1) * width] = dot(hot, packed_ref[...], TN).astype(BF16)


def final(choice, packed, experts, name):
    width = packed.shape[1] * PIECES
    return pl.pallas_call(
        functools.partial(final_kernel, experts),
        out_shape=jax.ShapeDtypeStruct((choice.shape[1], width), BF16),
        compiler_params=PARAMS,
        cost_estimate=COST,
        name=name,
    )(choice, packed)


def exchange(x, axis, parts, name):
    shaped = x.reshape(parts, x.shape[0] // parts, x.shape[1])
    with jax.named_scope(name):
        shaped = lax.all_to_all(shaped, axis, split_axis=0, concat_axis=0, tiled=True)
    return shaped.reshape(x.shape)


def after(x, *gates):
    return lax.optimization_barrier((x, *gates))[0]


def local(tokens, grad_out, router_weight, expert_choice, gate_pre, up_pre, w_gate, w_up, w_down):
    width = tokens.shape[1]
    experts = router_weight.shape[1]
    n_expert = lax.axis_size("expert")
    n_etp = lax.axis_size("etp")
    chips = n_etp // 2
    choice = expert_choice.reshape(1, -1)
    hidden = gate_pre.shape[2]
    slots = gate_pre.shape[1] // n_etp
    gate = gate_pre.reshape(n_etp, slots, hidden)
    up = up_pre.reshape(n_etp, slots, hidden)
    weights = (w_down[0], w_gate[0], w_up[0])
    mine = lax.axis_index("etp")
    core = mine % 2
    chip = mine // 2
    router = lax.dynamic_index_in_dim(router_weight.T, lax.axis_index("expert"), 0)
    near = (chip + jnp.array(HOPS, jnp.int32)) % chips * 2
    ids = jnp.stack([near + core, near + 1 - core], axis=1).reshape(-1).astype(jnp.int32)
    choice, ids, router = lax.optimization_barrier((choice, ids, router))

    def shift(x, by, name):
        with jax.named_scope(name):
            return lax.ppermute(x, "etp", [(i, ((i // 2 + by) % chips) * 2 + i % 2) for i in range(n_etp)])

    def swap(x, name):
        with jax.named_scope(name):
            return lax.ppermute(x, "etp", [(i, i ^ 1) for i in range(n_etp)])

    every = tuple(range(GROUPS))
    sent = pack(choice, grad_out, experts, every, "pack_grad")
    arrived = exchange(sent, "expert", n_expert, "grads")
    sent_tok = pack(choice, after(tokens, sent), experts, every, "pack_tok")
    halves = unpack(after(arrived, sent_tok), every, slots, 2, "unpack_grad")

    left = [shift(part, 1, f"left{i}") for i, part in enumerate(halves)]
    right = [shift(halves[i], -1, f"right{i}") for i in (1, 0)][::-1]
    own_x = [swap(part, f"own_x{i}") for i, part in enumerate(halves)]
    packed_tok = exchange(after(sent_tok, own_x[0]), "expert", n_expert, "toks")
    own = [after(halves[0], sent_tok), halves[1]]
    keep, other = expert(ids, 0, [own + own_x], gate, up, *weights, "expert_own")
    keep_r = swap(other, "own_sum")
    left[0], right[1] = after(left[0], keep), after(right[1], keep)
    far = [shift(left[0], 1, "far0"), shift(right[1], -1, "far1")]
    left_x = [swap(part, f"left_x{i}") for i, part in enumerate(left)]
    right_x = [swap(part, f"right_x{i}") for i, part in enumerate(right)]
    lk, lo, rk, ro = expert(ids, 1, [left + left_x, right + right_x], gate, up, *weights, "expert_sides")
    lr, rr = swap(lo, "left_sum"), swap(ro, "right_sum")
    half = slots // 2
    first = add(half, "sum_left0", (lk, 0), (lr, 0)), add(half, "sum_right1", (rk, half), (rr, half))
    far = [after(far[0], lk), after(far[1], lk)]
    far_x = [swap(part, f"far_x{i}") for i, part in enumerate(far)]
    far = [after(far[0], *first), far[1]]
    fk, fo = expert(ids, 3, [far + far_x], gate, up, *weights, "expert_far")
    fr = swap(after(fo, packed_tok), "far_sum")

    to_left = [shift(first[0], -1, "to_left0"), None]
    to_right = [None, shift(first[1], 1, "to_right1")]
    sums = add(half, "sum_far0", (fk, 0), (fr, 0)), add(half, "sum_far1", (fk, half), (fr, half))
    via_right, via_left = shift(sums[0], 1, "via_right"), shift(sums[1], -1, "via_left")
    tok = unpack(after(packed_tok, *sums), every, slots, 2, "unpack_tok")
    gated_r, gated_l, *_ = lax.optimization_barrier((rk, lk, tok[0], to_left[0], to_right[1]))
    to_right[0] = shift(add(half, "sum_right0", (gated_r, 0), (rr, 0), (via_right, 0)), 1, "to_right0")
    to_left[1] = shift(add(half, "sum_left1", (gated_l, half), (lr, half), (via_left, 0)), -1, "to_left1")
    parts = [[to_right[h], to_left[h]] for h in range(2)]
    back, column = token_math([keep, keep_r], parts, tok, router, "token_math")
    returned = exchange(back, "expert", n_expert, "back")
    token_grad = final(choice, returned, experts, "final")

    bit = 1
    while bit < n_etp:
        column = column + lax.ppermute(column, "etp", [(i, i ^ bit) for i in range(n_etp)])
        bit *= 2
    column = after(column, returned).astype(BF16).reshape(1, PIECES, width // PIECES)
    spread = jnp.broadcast_to(column, (n_expert, PIECES, width // PIECES))
    spread = lax.all_to_all(spread, "expert", split_axis=0, concat_axis=0, tiled=True)
    return (token_grad, spread.reshape(experts, width).astype(F32).T)


def solution(mesh):
    placed = (
        P(("expert", "etp"), None),
        P(("expert", "etp"), None),
        P(),
        P(("expert", "etp"), None),
        P("expert", None, "etp"),
        P("expert", None, "etp"),
        P("expert", None, "etp"),
        P("expert", None, "etp"),
        P("expert", "etp", None),
    )
    return jax.shard_map(
        local,
        mesh=mesh,
        in_specs=placed,
        out_specs=(P(("expert", "etp"), None), P()),
        check_vma=False,
    )
```

```python
import functools

import jax
import jax.numpy as jnp
from jax import lax
from jax.experimental import pallas as pl
from jax.experimental.pallas import tpu as pltpu
from jax.sharding import PartitionSpec as P

CAP = 6
PIECES = 4
GROUPS = 3
TILE = 8
NT = (((1,), (1,)), ((), ()))
TN = (((0,), (0,)), ((), ()))
NN = (((1,), (0,)), ((), ()))
F32 = jnp.float32
BF16 = jnp.bfloat16
PARAMS = pltpu.CompilerParams(vmem_limit_bytes=24 * 2**20)
COLUMNS = 512
HOPS = (0, -1, 1, 2)
COST = pl.CostEstimate(flops=0, transcendentals=0, bytes_accessed=2**20)


def iota(shape, axis):
    return lax.broadcasted_iota(jnp.int32, shape, axis)


def dot(a, b, dims=NN):
    return lax.dot_general(a, b, dims, preferred_element_type=F32)


def target_row(choice, experts):
    count = choice.shape[1]
    picked = (iota((experts, count), 0) == choice).astype(BF16)
    before = (iota((count, count), 0) < iota((count, count), 1)).astype(BF16)
    earlier = dot(picked, before)
    position = jnp.sum(picked.astype(F32) * earlier, axis=0, keepdims=True)
    return choice * CAP + position.astype(jnp.int32)


def hot_rows(target, peers, groups, piece):
    shape = (peers, len(groups) * TILE, target.shape[1])
    row = iota(shape, 1)
    slot = iota(shape, 0) * CAP + groups[0] * 2 + (row >> 3) * 2 + (row & 1)
    hit = (slot == target.reshape(1, 1, -1)) & (((row >> 1) & (PIECES - 1)) == piece)
    return jnp.where(hit, 1.0, 0.0).reshape(-1, target.shape[1]).astype(BF16)


def pack_rows(rows, target, peers, groups):
    width = rows.shape[1] // PIECES
    total = 0.0
    for piece in range(PIECES):
        total = total + dot(hot_rows(target, peers, groups, piece), rows[:, piece * width : (piece + 1) * width])
    return total.astype(BF16)


def pack_kernel(experts, groups, choice_ref, rows_ref, out_ref):
    target = target_row(choice_ref[...], experts)
    out_ref[...] = pack_rows(rows_ref[...], target, experts, groups)


def pack(choice, rows, experts, groups, name):
    width = rows.shape[1] // PIECES
    return pl.pallas_call(
        functools.partial(pack_kernel, experts, groups),
        out_shape=jax.ShapeDtypeStruct((experts * len(groups) * TILE, width), BF16),
        compiler_params=PARAMS,
        cost_estimate=COST,
        name=name,
    )(choice, rows)


def unpack_kernel(groups, packed_ref, *outs):
    width = packed_ref.shape[1]
    take = packed_ref.shape[0] // len(outs)
    rows = outs[0].shape[0]
    target = iota((1, rows), 1)
    for piece in range(PIECES):
        hot = hot_rows(target, rows // CAP, groups, piece)
        for half, out in enumerate(outs):
            part = packed_ref[half * take : (half + 1) * take, :]
            out[:, piece * width : (piece + 1) * width] = dot(hot, part, TN).astype(BF16)


def unpack(packed, groups, slots, halves, name):
    width = packed.shape[1] * PIECES
    return pl.pallas_call(
        functools.partial(unpack_kernel, groups),
        out_shape=[jax.ShapeDtypeStruct((slots // halves, width), BF16)] * halves,
        compiler_params=PARAMS,
        cost_estimate=COST,
        name=name,
    )(packed)


def expert_kernel(first, counts, ids_ref, *refs):
    total = sum(len(c) for c in counts)
    pieces, (gate_ref, up_ref, down_ref, wg_ref, wu_ref) = refs[:total], refs[total : total + 5]
    outs = refs[total + 5 : total + 5 + 2 * len(counts)]
    lhs_ref, out_ref, dg_ref, du_ref, in_sem, out_sem = refs[total + 5 + len(outs) :]
    slots, width = outs[0].shape
    copies, at, number = [], 0, 0
    for chip in counts:
        for rows in chip:
            copies.append(pltpu.make_async_copy(pieces[number], lhs_ref.at[pl.ds(at, rows)], in_sem.at[number]))
            at, number = at + rows, number + 1
    for copy in copies:
        copy.start()
    last, number = [], 0
    for j, chip in enumerate(counts):
        spot = pl.ds(j * 2 * slots, 2 * slots)
        for _ in chip:
            copies[number].wait()
            number += 1
        hidden = dot(lhs_ref[spot, :], down_ref[...], NT)
        own, peer = ids_ref[2 * (first + j)], ids_ref[2 * (first + j) + 1]
        gate = jnp.concatenate([gate_ref[own], gate_ref[peer]], axis=0).astype(F32)
        up = jnp.concatenate([up_ref[own], up_ref[peer]], axis=0).astype(F32)
        sig = jax.nn.sigmoid(gate)
        dg_ref[...] = (hidden * up * sig * (1.0 + gate * (1.0 - sig))).astype(BF16)
        du_ref[...] = (hidden * gate * sig).astype(BF16)

        def tile(at):
            cols = pl.ds(at, COLUMNS)
            terms = dot(dg_ref[...], wg_ref[cols, :], NT) + dot(du_ref[...], wu_ref[cols, :], NT)
            out_ref[spot, cols] = terms.astype(BF16)

        if first == HOPS.index(2):
            for i in range(width // COLUMNS):
                tile(i * COLUMNS)
        else:

            @pl.loop(0, width // COLUMNS)
            def _(i):
                tile(pl.multiple_of(i * COLUMNS, COLUMNS))

        for i in range(2 * j, 2 * j + 2):
            copy = pltpu.make_async_copy(out_ref.at[pl.ds(i * slots, slots)], outs[i], out_sem.at[i])
            copy.start()
            last.append(copy)
    for copy in last:
        copy.wait()


def expert(ids, first, chips, gate, up, down_w, gate_w, up_w, name):
    width = chips[0][0].shape[1]
    slots, hidden = gate.shape[1:]
    blocks = 2 * len(chips)
    counts = tuple(tuple(piece.shape[0] for piece in chip) for chip in chips)
    pieces = [piece for chip in chips for piece in chip]
    vmem = lambda *shape: pltpu.VMEM(shape, BF16)
    anywhere = pl.BlockSpec(memory_space=pl.ANY)
    held = pl.BlockSpec(memory_space=pltpu.VMEM)
    return pl.pallas_call(
        functools.partial(expert_kernel, first, counts),
        in_specs=[pl.BlockSpec(memory_space=pltpu.SMEM)] + [anywhere] * len(pieces) + [held] * 5,
        out_specs=[anywhere] * blocks,
        out_shape=[jax.ShapeDtypeStruct((slots, width), BF16)] * blocks,
        scratch_shapes=[
            vmem(blocks * slots, width), vmem(blocks * slots, width), vmem(2 * slots, hidden), vmem(2 * slots, hidden),
            pltpu.SemaphoreType.DMA((len(pieces),)), pltpu.SemaphoreType.DMA((blocks,)),
        ],
        compiler_params=pltpu.CompilerParams(vmem_limit_bytes=24 * 2**20),
        cost_estimate=pl.CostEstimate(flops=0, transcendentals=0, bytes_accessed=2**20),
        name=name,
    )(ids, *pieces, gate, up, down_w, gate_w, up_w)


def add_kernel(spots, *refs):
    parts, out_ref, held, sem = refs[: len(spots)], refs[len(spots)], refs[len(spots) + 1 : -1], refs[-1]
    copies = []
    for i, (start, part) in enumerate(zip(spots, parts)):
        copies.append(pltpu.make_async_copy(part.at[pl.ds(start, held[i].shape[0])], held[i], sem.at[i]))
    for copy in copies:
        copy.start()
    for copy in copies:
        copy.wait()
    out_ref[...] = sum(ref[...].astype(F32) for ref in held).astype(BF16)


def add(rows, name, *parts):
    width = parts[0][0].shape[1]
    return pl.pallas_call(
        functools.partial(add_kernel, tuple(start for _, start in parts)),
        in_specs=[pl.BlockSpec(memory_space=pl.ANY)] * len(parts),
        out_shape=jax.ShapeDtypeStruct((rows, width), BF16),
        scratch_shapes=[pltpu.VMEM((rows, width), BF16)] * len(parts) + [pltpu.SemaphoreType.DMA((len(parts),))],
        compiler_params=pltpu.CompilerParams(vmem_limit_bytes=12 * 2**20),
        cost_estimate=COST,
        name=name,
    )(*[part for part, _ in parts])


def token_kernel(router_ref, keep_ref, keep_r_ref, *refs):
    parts, toks, (out_ref, column_ref) = refs[:4], refs[4:6], refs[6:]
    router = router_ref[...].astype(F32)
    column, grads = 0.0, []
    rows = toks[0].shape[0]
    take = out_ref.shape[0] // 2
    for half in range(2):
        spot = slice(half * rows, (half + 1) * rows)
        total = keep_ref[spot, :].astype(F32) + keep_r_ref[spot, :].astype(F32)
        for part in parts[2 * half : 2 * half + 2]:
            total = total + part[...].astype(F32)
        grad = total.astype(BF16).astype(F32)
        tok = toks[half][...].astype(F32)
        score = jax.nn.sigmoid(jnp.sum(tok * router, axis=1, keepdims=True))
        d_logit = jnp.sum(tok * grad, axis=1, keepdims=True) * score * (1.0 - score)
        token_grad = (score * grad + d_logit * router).astype(BF16)
        column = column + jnp.sum(d_logit * tok, axis=0, keepdims=True)
        grads.append(token_grad)
    column_ref[...] = column
    width = out_ref.shape[1]
    packed = [0.0, 0.0]
    for piece in range(PIECES):
        hot = hot_rows(iota((1, rows), 1), rows // CAP, tuple(range(GROUPS)), piece)
        for half in range(2):
            packed[half] = packed[half] + dot(hot, grads[half][:, piece * width : (piece + 1) * width])
    for half in range(2):
        out_ref[half * take : (half + 1) * take, :] = packed[half].astype(BF16)


def token_math(kept, parts, tok, router, name):
    rows, width = tok[0].shape
    return pl.pallas_call(
        token_kernel,
        out_shape=[
            jax.ShapeDtypeStruct((2 * rows // CAP * GROUPS * TILE, width // PIECES), BF16),
            jax.ShapeDtypeStruct((1, width), F32),
        ],
        compiler_params=PARAMS,
        cost_estimate=COST,
        name=name,
    )(router, *kept, *parts[0], *parts[1], *tok)


def final_kernel(experts, choice_ref, packed_ref, out_ref):
    target = target_row(choice_ref[...], experts)
    width = packed_ref.shape[1]
    for piece in range(PIECES):
        hot = hot_rows(target, experts, tuple(range(GROUPS)), piece)
        out_ref[:, piece * width : (piece + 1) * width] = dot(hot, packed_ref[...], TN).astype(BF16)


def final(choice, packed, experts, name):
    width = packed.shape[1] * PIECES
    return pl.pallas_call(
        functools.partial(final_kernel, experts),
        out_shape=jax.ShapeDtypeStruct((choice.shape[1], width), BF16),
        compiler_params=PARAMS,
        cost_estimate=COST,
        name=name,
    )(choice, packed)


def exchange(x, axis, parts, name):
    shaped = x.reshape(parts, x.shape[0] // parts, x.shape[1])
    with jax.named_scope(name):
        shaped = lax.all_to_all(shaped, axis, split_axis=0, concat_axis=0, tiled=True)
    return shaped.reshape(x.shape)


def after(x, *gates):
    return lax.optimization_barrier((x, *gates))[0]


def local(tokens, grad_out, router_weight, expert_choice, gate_pre, up_pre, w_gate, w_up, w_down):
    width = tokens.shape[1]
    experts = router_weight.shape[1]
    n_expert = lax.axis_size("expert")
    n_etp = lax.axis_size("etp")
    chips = n_etp // 2
    choice = expert_choice.reshape(1, -1)
    hidden = gate_pre.shape[2]
    slots = gate_pre.shape[1] // n_etp
    gate = gate_pre.reshape(n_etp, slots, hidden)
    up = up_pre.reshape(n_etp, slots, hidden)
    weights = (w_down[0], w_gate[0], w_up[0])
    mine = lax.axis_index("etp")
    core = mine % 2
    chip = mine // 2
    router = lax.dynamic_index_in_dim(router_weight.T, lax.axis_index("expert"), 0)
    near = (chip + jnp.array(HOPS, jnp.int32)) % chips * 2
    ids = jnp.stack([near + core, near + 1 - core], axis=1).reshape(-1).astype(jnp.int32)
    choice, ids, router = lax.optimization_barrier((choice, ids, router))

    def shift(x, by, name):
        with jax.named_scope(name):
            return lax.ppermute(x, "etp", [(i, ((i // 2 + by) % chips) * 2 + i % 2) for i in range(n_etp)])

    def swap(x, name):
        with jax.named_scope(name):
            return lax.ppermute(x, "etp", [(i, i ^ 1) for i in range(n_etp)])

    every = tuple(range(GROUPS))
    sent = pack(choice, grad_out, experts, every, "pack_grad")
    arrived = exchange(sent, "expert", n_expert, "grads")
    sent_tok = pack(choice, after(tokens, sent), experts, every, "pack_tok")
    halves = unpack(after(arrived, sent_tok), every, slots, 2, "unpack_grad")

    left = [shift(part, 1, f"left{i}") for i, part in enumerate(halves)]
    right = [shift(halves[i], -1, f"right{i}") for i in (1, 0)][::-1]
    own_x = [swap(part, f"own_x{i}") for i, part in enumerate(halves)]
    packed_tok = exchange(after(sent_tok, own_x[0]), "expert", n_expert, "toks")
    own = [after(halves[0], sent_tok), halves[1]]
    keep, other = expert(ids, 0, [own + own_x], gate, up, *weights, "expert_own")
    keep_r = swap(other, "own_sum")
    left[0], right[1] = after(left[0], keep), after(right[1], keep)
    far = [shift(left[0], 1, "far0"), shift(right[1], -1, "far1")]
    left_x = [swap(part, f"left_x{i}") for i, part in enumerate(left)]
    right_x = [swap(part, f"right_x{i}") for i, part in enumerate(right)]
    lk, lo, rk, ro = expert(ids, 1, [left + left_x, right + right_x], gate, up, *weights, "expert_sides")
    lr, rr = swap(lo, "left_sum"), swap(ro, "right_sum")
    half = slots // 2
    first = add(half, "sum_left0", (lk, 0), (lr, 0)), add(half, "sum_right1", (rk, half), (rr, half))
    far = [after(far[0], lk), after(far[1], lk)]
    far_x = [swap(part, f"far_x{i}") for i, part in enumerate(far)]
    far = [after(far[0], *first), far[1]]
    fk, fo = expert(ids, 3, [far + far_x], gate, up, *weights, "expert_far")
    fr = swap(after(fo, packed_tok), "far_sum")

    to_left = [shift(first[0], -1, "to_left0"), None]
    to_right = [None, shift(first[1], 1, "to_right1")]
    sums = add(half, "sum_far0", (fk, 0), (fr, 0)), add(half, "sum_far1", (fk, half), (fr, half))
    via_right, via_left = shift(sums[0], 1, "via_right"), shift(sums[1], -1, "via_left")
    tok = unpack(after(packed_tok, *sums), every, slots, 2, "unpack_tok")
    gated_r, gated_l, *_ = lax.optimization_barrier((rk, lk, tok[0], to_left[0], to_right[1]))
    to_right[0] = shift(add(half, "sum_right0", (gated_r, 0), (rr, 0), (via_right, 0)), 1, "to_right0")
    to_left[1] = shift(add(half, "sum_left1", (gated_l, half), (lr, half), (via_left, 0)), -1, "to_left1")
    parts = [[to_right[h], to_left[h]] for h in range(2)]
    back, column = token_math([keep, keep_r], parts, tok, router, "token_math")
    returned = exchange(back, "expert", n_expert, "back")
    token_grad = final(choice, returned, experts, "final")

    bit = 1
    while bit < n_etp:
        column = column + lax.ppermute(column, "etp", [(i, i ^ bit) for i in range(n_etp)])
        bit *= 2
    column = after(column, returned).astype(BF16).reshape(1, PIECES, width // PIECES)
    spread = jnp.broadcast_to(column, (n_expert, PIECES, width // PIECES))
    spread = lax.all_to_all(spread, "expert", split_axis=0, concat_axis=0, tiled=True)
    return (token_grad, spread.reshape(experts, width).astype(F32).T)


def solution(mesh):
    placed = (
        P(("expert", "etp"), None),
        P(("expert", "etp"), None),
        P(),
        P(("expert", "etp"), None),
        P("expert", None, "etp"),
        P("expert", None, "etp"),
        P("expert", None, "etp"),
        P("expert", None, "etp"),
        P("expert", "etp", None),
    )
    return jax.shard_map(
        local,
        mesh=mesh,
        in_specs=placed,
        out_specs=(P(("expert", "etp"), None), P()),
        check_vma=False,
    )
```

```python
import functools

import jax
import jax.numpy as jnp
from jax import lax
from jax.experimental import pallas as pl
from jax.experimental.pallas import tpu as pltpu
from jax.sharding import PartitionSpec as P

CAP = 6
PIECES = 4
GROUPS = 3
TILE = 8
NT = (((1,), (1,)), ((), ()))
TN = (((0,), (0,)), ((), ()))
NN = (((1,), (0,)), ((), ()))
F32 = jnp.float32
BF16 = jnp.bfloat16
PARAMS = pltpu.CompilerParams(vmem_limit_bytes=24 * 2**20)
COLUMNS = 512
EARLY = ("sum_left0", "sum_right1")
HOPS = (0, -1, 1, 2)
COST = pl.CostEstimate(flops=0, transcendentals=0, bytes_accessed=2**20)


def iota(shape, axis):
    return lax.broadcasted_iota(jnp.int32, shape, axis)


def dot(a, b, dims=NN):
    return lax.dot_general(a, b, dims, preferred_element_type=F32)


def target_row(choice, experts):
    count = choice.shape[1]
    picked = (iota((experts, count), 0) == choice).astype(BF16)
    before = (iota((count, count), 0) < iota((count, count), 1)).astype(BF16)
    earlier = dot(picked, before)
    position = jnp.sum(picked.astype(F32) * earlier, axis=0, keepdims=True)
    return choice * CAP + position.astype(jnp.int32)


def hot_rows(target, peers, groups, piece):
    shape = (peers, len(groups) * TILE, target.shape[1])
    row = iota(shape, 1)
    slot = iota(shape, 0) * CAP + groups[0] * 2 + (row >> 3) * 2 + (row & 1)
    hit = (slot == target.reshape(1, 1, -1)) & (((row >> 1) & (PIECES - 1)) == piece)
    return jnp.where(hit, 1.0, 0.0).reshape(-1, target.shape[1]).astype(BF16)


def pack_rows(rows, target, peers, groups):
    width = rows.shape[1] // PIECES
    total = 0.0
    for piece in range(PIECES):
        total = total + dot(hot_rows(target, peers, groups, piece), rows[:, piece * width : (piece + 1) * width])
    return total.astype(BF16)


def pack_kernel(experts, groups, choice_ref, rows_ref, out_ref):
    target = target_row(choice_ref[...], experts)
    out_ref[...] = pack_rows(rows_ref[...], target, experts, groups)


def pack(choice, rows, experts, groups, name):
    width = rows.shape[1] // PIECES
    return pl.pallas_call(
        functools.partial(pack_kernel, experts, groups),
        out_shape=jax.ShapeDtypeStruct((experts * len(groups) * TILE, width), BF16),
        compiler_params=PARAMS,
        cost_estimate=COST,
        name=name,
    )(choice, rows)


def unpack_kernel(groups, packed_ref, *outs):
    width = packed_ref.shape[1]
    take = packed_ref.shape[0] // len(outs)
    rows = outs[0].shape[0]
    target = iota((1, rows), 1)
    for piece in range(PIECES):
        hot = hot_rows(target, rows // CAP, groups, piece)
        for half, out in enumerate(outs):
            part = packed_ref[half * take : (half + 1) * take, :]
            out[:, piece * width : (piece + 1) * width] = dot(hot, part, TN).astype(BF16)


def unpack(packed, groups, slots, halves, name):
    width = packed.shape[1] * PIECES
    return pl.pallas_call(
        functools.partial(unpack_kernel, groups),
        out_shape=[jax.ShapeDtypeStruct((slots // halves, width), BF16)] * halves,
        compiler_params=PARAMS,
        cost_estimate=COST,
        name=name,
    )(packed)


def expert_kernel(first, counts, ids_ref, *refs):
    total = sum(len(c) for c in counts)
    pieces, (gate_ref, up_ref, down_ref, wg_ref, wu_ref) = refs[:total], refs[total : total + 5]
    outs = refs[total + 5 : total + 5 + 2 * len(counts)]
    lhs_ref, out_ref, dg_ref, du_ref, in_sem, out_sem = refs[total + 5 + len(outs) :]
    slots, width = outs[0].shape
    copies, at, number = [], 0, 0
    for chip in counts:
        for rows in chip:
            copies.append(pltpu.make_async_copy(pieces[number], lhs_ref.at[pl.ds(at, rows)], in_sem.at[number]))
            at, number = at + rows, number + 1
    for copy in copies:
        copy.start()
    last, number = [], 0
    for j, chip in enumerate(counts):
        spot = pl.ds(j * 2 * slots, 2 * slots)
        for _ in chip:
            copies[number].wait()
            number += 1
        hidden = dot(lhs_ref[spot, :], down_ref[...], NT)
        own, peer = ids_ref[2 * (first + j)], ids_ref[2 * (first + j) + 1]
        gate = jnp.concatenate([gate_ref[own], gate_ref[peer]], axis=0).astype(F32)
        up = jnp.concatenate([up_ref[own], up_ref[peer]], axis=0).astype(F32)
        sig = jax.nn.sigmoid(gate)
        dg_ref[...] = (hidden * up * sig * (1.0 + gate * (1.0 - sig))).astype(BF16)
        du_ref[...] = (hidden * gate * sig).astype(BF16)

        def tile(at):
            cols = pl.ds(at, COLUMNS)
            terms = dot(dg_ref[...], wg_ref[cols, :], NT) + dot(du_ref[...], wu_ref[cols, :], NT)
            out_ref[spot, cols] = terms.astype(BF16)

        if first == HOPS.index(2):
            for i in range(width // COLUMNS):
                tile(i * COLUMNS)
        else:

            @pl.loop(0, width // COLUMNS)
            def _(i):
                tile(pl.multiple_of(i * COLUMNS, COLUMNS))

        for i in range(2 * j, 2 * j + 2):
            copy = pltpu.make_async_copy(out_ref.at[pl.ds(i * slots, slots)], outs[i], out_sem.at[i])
            copy.start()
            last.append(copy)
    for copy in last:
        copy.wait()


def expert(ids, first, chips, gate, up, down_w, gate_w, up_w, name):
    width = chips[0][0].shape[1]
    slots, hidden = gate.shape[1:]
    blocks = 2 * len(chips)
    counts = tuple(tuple(piece.shape[0] for piece in chip) for chip in chips)
    pieces = [piece for chip in chips for piece in chip]
    vmem = lambda *shape: pltpu.VMEM(shape, BF16)
    anywhere = pl.BlockSpec(memory_space=pl.ANY)
    held = pl.BlockSpec(memory_space=pltpu.VMEM)
    return pl.pallas_call(
        functools.partial(expert_kernel, first, counts),
        in_specs=[pl.BlockSpec(memory_space=pltpu.SMEM)] + [anywhere] * len(pieces) + [held] * 5,
        out_specs=[anywhere] * blocks,
        out_shape=[jax.ShapeDtypeStruct((slots, width), BF16)] * blocks,
        scratch_shapes=[
            vmem(blocks * slots, width), vmem(blocks * slots, width), vmem(2 * slots, hidden), vmem(2 * slots, hidden),
            pltpu.SemaphoreType.DMA((len(pieces),)), pltpu.SemaphoreType.DMA((blocks,)),
        ],
        compiler_params=pltpu.CompilerParams(vmem_limit_bytes=24 * 2**20),
        cost_estimate=pl.CostEstimate(flops=0, transcendentals=0, bytes_accessed=2**20),
        name=name,
    )(ids, *pieces, gate, up, down_w, gate_w, up_w)


def add_kernel(spots, *refs):
    parts, out_ref, held, sem = refs[: len(spots)], refs[len(spots)], refs[len(spots) + 1 : -1], refs[-1]
    copies = []
    for i, (start, part) in enumerate(zip(spots, parts)):
        copies.append(pltpu.make_async_copy(part.at[pl.ds(start, held[i].shape[0])], held[i], sem.at[i]))
    for copy in copies:
        copy.start()
    for copy in copies:
        copy.wait()
    out_ref[...] = sum(ref[...].astype(F32) for ref in held).astype(BF16)


def add(rows, name, *parts):
    width = parts[0][0].shape[1]
    return pl.pallas_call(
        functools.partial(add_kernel, tuple(start for _, start in parts)),
        in_specs=[pl.BlockSpec(memory_space=pl.ANY)] * len(parts),
        out_shape=jax.ShapeDtypeStruct((rows, width), BF16),
        scratch_shapes=[pltpu.VMEM((rows, width), BF16)] * len(parts) + [pltpu.SemaphoreType.DMA((len(parts),))],
        compiler_params=pltpu.CompilerParams(vmem_limit_bytes=(12 if name in EARLY else 56) * 2**20),
        cost_estimate=COST,
        name=name,
    )(*[part for part, _ in parts])


def token_kernel(router_ref, keep_ref, keep_r_ref, *refs):
    parts, toks, (out_ref, column_ref) = refs[:4], refs[4:6], refs[6:]
    router = router_ref[...].astype(F32)
    column, grads = 0.0, []
    rows = toks[0].shape[0]
    take = out_ref.shape[0] // 2
    for half in range(2):
        spot = slice(half * rows, (half + 1) * rows)
        total = keep_ref[spot, :].astype(F32) + keep_r_ref[spot, :].astype(F32)
        for part in parts[2 * half : 2 * half + 2]:
            total = total + part[...].astype(F32)
        grad = total.astype(BF16).astype(F32)
        tok = toks[half][...].astype(F32)
        score = jax.nn.sigmoid(jnp.sum(tok * router, axis=1, keepdims=True))
        d_logit = jnp.sum(tok * grad, axis=1, keepdims=True) * score * (1.0 - score)
        token_grad = (score * grad + d_logit * router).astype(BF16)
        column = column + jnp.sum(d_logit * tok, axis=0, keepdims=True)
        grads.append(token_grad)
    column_ref[...] = column
    width = out_ref.shape[1]
    packed = [0.0, 0.0]
    for piece in range(PIECES):
        hot = hot_rows(iota((1, rows), 1), rows // CAP, tuple(range(GROUPS)), piece)
        for half in range(2):
            packed[half] = packed[half] + dot(hot, grads[half][:, piece * width : (piece + 1) * width])
    for half in range(2):
        out_ref[half * take : (half + 1) * take, :] = packed[half].astype(BF16)


def token_math(kept, parts, tok, router, name):
    rows, width = tok[0].shape
    return pl.pallas_call(
        token_kernel,
        out_shape=[
            jax.ShapeDtypeStruct((2 * rows // CAP * GROUPS * TILE, width // PIECES), BF16),
            jax.ShapeDtypeStruct((1, width), F32),
        ],
        compiler_params=PARAMS,
        cost_estimate=COST,
        name=name,
    )(router, *kept, *parts[0], *parts[1], *tok)


def final_kernel(experts, choice_ref, packed_ref, out_ref):
    target = target_row(choice_ref[...], experts)
    width = packed_ref.shape[1]
    for piece in range(PIECES):
        hot = hot_rows(target, experts, tuple(range(GROUPS)), piece)
        out_ref[:, piece * width : (piece + 1) * width] = dot(hot, packed_ref[...], TN).astype(BF16)


def final(choice, packed, experts, name):
    width = packed.shape[1] * PIECES
    return pl.pallas_call(
        functools.partial(final_kernel, experts),
        out_shape=jax.ShapeDtypeStruct((choice.shape[1], width), BF16),
        compiler_params=PARAMS,
        cost_estimate=COST,
        name=name,
    )(choice, packed)


def exchange(x, axis, parts, name):
    shaped = x.reshape(parts, x.shape[0] // parts, x.shape[1])
    with jax.named_scope(name):
        shaped = lax.all_to_all(shaped, axis, split_axis=0, concat_axis=0, tiled=True)
    return shaped.reshape(x.shape)


def after(x, *gates):
    return lax.optimization_barrier((x, *gates))[0]


def local(tokens, grad_out, router_weight, expert_choice, gate_pre, up_pre, w_gate, w_up, w_down):
    width = tokens.shape[1]
    experts = router_weight.shape[1]
    n_expert = lax.axis_size("expert")
    n_etp = lax.axis_size("etp")
    chips = n_etp // 2
    choice = expert_choice.reshape(1, -1)
    hidden = gate_pre.shape[2]
    slots = gate_pre.shape[1] // n_etp
    gate = gate_pre.reshape(n_etp, slots, hidden)
    up = up_pre.reshape(n_etp, slots, hidden)
    weights = (w_down[0], w_gate[0], w_up[0])
    mine = lax.axis_index("etp")
    core = mine % 2
    chip = mine // 2
    router = lax.dynamic_index_in_dim(router_weight.T, lax.axis_index("expert"), 0)
    near = (chip + jnp.array(HOPS, jnp.int32)) % chips * 2
    ids = jnp.stack([near + core, near + 1 - core], axis=1).reshape(-1).astype(jnp.int32)
    choice, ids, router = lax.optimization_barrier((choice, ids, router))

    def shift(x, by, name):
        with jax.named_scope(name):
            return lax.ppermute(x, "etp", [(i, ((i // 2 + by) % chips) * 2 + i % 2) for i in range(n_etp)])

    def swap(x, name):
        with jax.named_scope(name):
            return lax.ppermute(x, "etp", [(i, i ^ 1) for i in range(n_etp)])

    every = tuple(range(GROUPS))
    sent = pack(choice, grad_out, experts, every, "pack_grad")
    arrived = exchange(sent, "expert", n_expert, "grads")
    sent_tok = pack(choice, after(tokens, sent), experts, every, "pack_tok")
    halves = unpack(after(arrived, sent_tok), every, slots, 2, "unpack_grad")

    left = [shift(part, 1, f"left{i}") for i, part in enumerate(halves)]
    right = [shift(halves[i], -1, f"right{i}") for i in (1, 0)][::-1]
    own_x = [swap(part, f"own_x{i}") for i, part in enumerate(halves)]
    packed_tok = exchange(after(sent_tok, own_x[0]), "expert", n_expert, "toks")
    own = [after(halves[0], sent_tok), halves[1]]
    keep, other = expert(ids, 0, [own + own_x], gate, up, *weights, "expert_own")
    keep_r = swap(other, "own_sum")
    left[0], right[1] = after(left[0], keep), after(right[1], keep)
    far = [shift(left[0], 1, "far0"), shift(right[1], -1, "far1")]
    left_x = [swap(part, f"left_x{i}") for i, part in enumerate(left)]
    right_x = [swap(part, f"right_x{i}") for i, part in enumerate(right)]
    lk, lo, rk, ro = expert(ids, 1, [left + left_x, right + right_x], gate, up, *weights, "expert_sides")
    lr, rr = swap(lo, "left_sum"), swap(ro, "right_sum")
    half = slots // 2
    first = add(half, "sum_left0", (lk, 0), (lr, 0)), add(half, "sum_right1", (rk, half), (rr, half))
    far = [after(far[0], lk), after(far[1], lk)]
    far_x = [swap(part, f"far_x{i}") for i, part in enumerate(far)]
    far = [after(far[0], *first), far[1]]
    fk, fo = expert(ids, 3, [far + far_x], gate, up, *weights, "expert_far")
    fr = swap(after(fo, packed_tok), "far_sum")

    to_left = [shift(first[0], -1, "to_left0"), None]
    to_right = [None, shift(first[1], 1, "to_right1")]
    sums = add(half, "sum_far0", (fk, 0), (fr, 0)), add(half, "sum_far1", (fk, half), (fr, half))
    via_right, via_left = shift(sums[0], 1, "via_right"), shift(sums[1], -1, "via_left")
    tok = unpack(after(packed_tok, *sums), every, slots, 2, "unpack_tok")
    gated_r, gated_l, *_ = lax.optimization_barrier((rk, lk, tok[0], to_left[0], to_right[1]))
    to_right[0] = shift(add(half, "sum_right0", (gated_r, 0), (rr, 0), (via_right, 0)), 1, "to_right0")
    to_left[1] = shift(add(half, "sum_left1", (gated_l, half), (lr, half), (via_left, 0)), -1, "to_left1")
    parts = [[to_right[h], to_left[h]] for h in range(2)]
    back, column = token_math([keep, keep_r], parts, tok, router, "token_math")
    returned = exchange(back, "expert", n_expert, "back")
    token_grad = final(choice, returned, experts, "final")

    bit = 1
    while bit < n_etp:
        column = column + lax.ppermute(column, "etp", [(i, i ^ bit) for i in range(n_etp)])
        bit *= 2
    column = after(column, returned).astype(BF16).reshape(1, PIECES, width // PIECES)
    spread = jnp.broadcast_to(column, (n_expert, PIECES, width // PIECES))
    spread = lax.all_to_all(spread, "expert", split_axis=0, concat_axis=0, tiled=True)
    return (token_grad, spread.reshape(experts, width).astype(F32).T)


def solution(mesh):
    placed = (
        P(("expert", "etp"), None),
        P(("expert", "etp"), None),
        P(),
        P(("expert", "etp"), None),
        P("expert", None, "etp"),
        P("expert", None, "etp"),
        P("expert", None, "etp"),
        P("expert", None, "etp"),
        P("expert", "etp", None),
    )
    return jax.shard_map(
        local,
        mesh=mesh,
        in_specs=placed,
        out_specs=(P(("expert", "etp"), None), P()),
        check_vma=False,
    )
```
